128 devices in a mesh: row: 8 (over x_hi, y), col: 16 (over z, x_lo, core).
Axes of the slice: x: 4 (x_hi: 2, x_lo: 2; x = x_hi * 2 + x_lo), y: 4, z: 4, core: 2. Of those that a mesh axis runs over, the one named last changes fastest.
Arguments:
- scalar: bfloat16 [512, 512, 512], P('row', 'col'), may hold values from -6 to 6
- register_in: float32 [512, 512, 512], P('row', 'col'), may hold values from -6 to 6
- drift_x: bfloat16 [512, 512, 512], P('row', 'col'), may hold values from -6 to 6
- drift_y: bfloat16 [512, 512, 512], P(None, 'col', 'row'), may hold values from -6 to 6
- drift_z: bfloat16 [512, 512, 512], P('row', 'col'), may hold values from -6 to 6
- diffusivity: bfloat16 [512, 512, 512], P('row', 'col'), may hold values from 0.099609375 to 1
- metric_x: float32 [512], replicated, may hold values from 0.5 to 2
- metric_y: float32 [512], replicated, may hold values from 0.5 to 2
- metric_z: float32 [512], replicated, may hold values from 0.5 to 2
- first_x: bfloat16 [512, 512], replicated, may hold values from -0.25 to 0.25
- second_x: bfloat16 [512, 512], replicated, may hold values from -0.25 to 0.25
- first_y: bfloat16 [512, 512], replicated, may hold values from -0.25 to 0.25
- second_y: bfloat16 [512, 512], replicated, may hold values from -0.25 to 0.25
- first_z: bfloat16 [512, 512], replicated, may hold values from -0.25 to 0.25
- second_z: bfloat16 [512, 512], replicated, may hold values from -0.25 to 0.25
Outputs:
- register_out: float32 [512, 512, 512], P('row', 'col')
- scalar_out: bfloat16 [512, 512, 512], P('row', 'col')
The draws below stay inside these ranges and needn't reach their ends.
All inputs are finite; a program needn't handle non-finite values.
Results may differ from the reference program's by a relative error of at most 0.001.
Values may be sent and summed in bfloat16 or wider, within the bound.
No kernel may reach another device: no remote copies, remote signals or barrier semaphores. Data moves between devices by JAX's collectives and lax.ppermute only.
A program may use at most 128 MiB of HBM per device.

```python
import math
import jax
import jax.numpy as jnp
from jax import lax

NX = 512
NY = 512
NZ = 512


def block_scale(stream_key, extent, cuts, smallest, high):
    factor_of = 1.0
    for axis_at, parts in cuts:
        steps = jax.random.uniform(jax.random.fold_in(jax.random.fold_in(stream_key, 6), axis_at), (parts,), jnp.float32, smallest / len(cuts), high / len(cuts))
        factor_of = factor_of * jnp.repeat(jnp.exp(steps), extent[axis_at] // parts).reshape((-1,) + (1,) * (len(extent) - 1 - axis_at))
    return factor_of


def bell_draw(own_key, shape, spread, bound, cuts=(), dtype=jnp.bfloat16):
    drawn = jax.random.normal(own_key, shape, jnp.float32) * spread
    if len(cuts) > 0:
        drawn = block_scale(own_key, shape, cuts, -0.22, 0.18) * drawn
    return jnp.clip(drawn, min=-bound, max=bound).astype(dtype)


def setup_inputs(seed: int = 0) -> dict:
    keys = jax.random.split(jax.random.key(seed), 16)
    return {
        "scalar": bell_draw(keys[0], (NY, NZ, NX), 1.0, 6.0, ((0, 8), (1, 16))),
        "register_in": bell_draw(keys[1], (NY, NZ, NX), 1.0, 6.0, ((0, 8), (1, 16)), jnp.float32),
        "drift_x": bell_draw(keys[2], (NY, NZ, NX), 1.0, 6.0, ((0, 8), (1, 16))),
        "drift_y": bell_draw(keys[3], (NY, NZ, NX), 1.0, 6.0, ((1, 16), (2, 8))),
        "drift_z": bell_draw(keys[4], (NY, NZ, NX), 1.0, 6.0, ((0, 8), (1, 16))),
        "diffusivity": jnp.clip(jnp.exp(math.log(1.0) - 2.306499 * jax.random.uniform(keys[5], (NY, NZ, NX), jnp.float32) ** block_scale(keys[5], (NY, NZ, NX), ((0, 8), (1, 16)), -0.2, 0.2)), 0.099609375, 1.0).astype(jnp.bfloat16),
        "metric_x": jnp.clip(jnp.exp(jax.random.uniform(keys[6], (NX,), jnp.float32, math.log(0.5), math.log(2.0))), 0.5, 2.0),
        "metric_y": jnp.clip(jnp.exp(jax.random.uniform(keys[7], (NY,), jnp.float32, math.log(0.5), math.log(2.0))), 0.5, 2.0),
        "metric_z": jnp.clip(jnp.exp(jax.random.uniform(keys[8], (NZ,), jnp.float32, math.log(0.5), math.log(2.0))), 0.5, 2.0),
        "first_x": bell_draw(keys[9], (NX, NX), NX ** -0.5, 0.25),
        "second_x": bell_draw(keys[10], (NX, NX), NX ** -0.5, 0.25),
        "first_y": bell_draw(keys[11], (NY, NY), NY ** -0.5, 0.25),
        "second_y": bell_draw(keys[12], (NY, NY), NY ** -0.5, 0.25),
        "first_z": bell_draw(keys[13], (NZ, NZ), NZ ** -0.5, 0.25),
        "second_z": bell_draw(keys[14], (NZ, NZ), NZ ** -0.5, 0.25),
    }


def reference(scalar, register_in, drift_x, drift_y, drift_z, diffusivity, metric_x, metric_y, metric_z, first_x, second_x, first_y, second_y, first_z, second_z):
    highest = lax.Precision.HIGHEST
    values = scalar.astype(jnp.float32)
    coeff = diffusivity.astype(jnp.float32)
    grad_x = jnp.einsum('jki,ai->jka', values, first_x.astype(jnp.float32), precision=highest)
    curv_x = jnp.einsum('jki,ai->jka', values, second_x.astype(jnp.float32), precision=highest)
    scale_x = metric_x[None, None, :]
    term_x = (drift_x.astype(jnp.float32) * scale_x) * grad_x + (coeff * (scale_x * scale_x)) * curv_x
    grad_y = jnp.einsum('jki,aj->aki', values, first_y.astype(jnp.float32), precision=highest)
    curv_y = jnp.einsum('jki,aj->aki', values, second_y.astype(jnp.float32), precision=highest)
    scale_y = metric_y[:, None, None]
    term_y = (drift_y.astype(jnp.float32) * scale_y) * grad_y + (coeff * (scale_y * scale_y)) * curv_y
    grad_z = jnp.einsum('jki,ak->jai', values, first_z.astype(jnp.float32), precision=highest)
    curv_z = jnp.einsum('jki,ak->jai', values, second_z.astype(jnp.float32), precision=highest)
    scale_z = metric_z[None, :, None]
    term_z = (drift_z.astype(jnp.float32) * scale_z) * grad_z + (coeff * (scale_z * scale_z)) * curv_z
    tendency = term_x + (term_y + term_z)
    register_out = (-5.0 / 9.0) * register_in + 0.5 * tendency
    scalar_out = (values + (15.0 / 16.0) * register_out).astype(jnp.bfloat16)
    return register_out, scalar_out
```

```python
import jax
import jax.numpy as jnp
from jax import lax
from jax.experimental import pallas as pl
from jax.experimental.pallas import tpu as pltpu
from jax.sharding import PartitionSpec as P

F32 = jnp.float32
BF16 = jnp.bfloat16
F16 = jnp.float16
VMEM_LIMIT = 60 * 1024 * 1024

NJ, NK, NI = 64, 32, 512
YB = 8
PIECE = YB * 64


def params():
    return pltpu.CompilerParams(vmem_limit_bytes=VMEM_LIMIT)


def pow_of(values):
    top = jnp.max(jnp.abs(values), axis=0, keepdims=True)
    top = jnp.max(top, axis=1, keepdims=True)
    return jnp.floor(jnp.log2(jnp.maximum(top, 1e-30)))


def pack_kernel(at, s_ref, row_ref, z0_ref, z1_ref, z2_ref, z3_ref):
    zc = at[0]
    for s, out in enumerate((z0_ref, z1_ref, z2_ref, z3_ref)):
        off = pl.multiple_of(lax.rem(zc + s, 4) * 128, 128)
        out[...] = s_ref[:, :, pl.ds(off, 128)]
    for c in range(4):
        chunk = s_ref[:, :, 128 * c : 128 * (c + 1)]
        top, bot = chunk[:, :16, :], chunk[:, 16:, :]
        row_ref[2 * c] = jnp.concatenate([top[:, :, :64], bot[:, :, :64]], axis=-1)
        row_ref[2 * c + 1] = jnp.concatenate([top[:, :, 64:], bot[:, :, 64:]], axis=-1)


def pack(at, scalar):
    jb = 16
    piece = jax.ShapeDtypeStruct((NJ, NK, 128), BF16)
    piece_spec = pl.BlockSpec((jb, NK, 128), lambda j, at: (j, 0, 0))
    return pl.pallas_call(
        pack_kernel,
        grid_spec=pltpu.PrefetchScalarGridSpec(
            num_scalar_prefetch=1,
            grid=(NJ // jb,),
            in_specs=[pl.BlockSpec((jb, NK, NI), lambda j, at: (j, 0, 0))],
            out_specs=[pl.BlockSpec((8, jb, 16, 128), lambda j, at: (0, j, 0, 0))] + [piece_spec] * 4,
        ),
        out_shape=[jax.ShapeDtypeStruct((8, NJ, 16, 128), BF16)] + [piece] * 4,
        compiler_params=params(),
        name="pack",
    )(at, scalar)


def operator_kernel(at, first_ref, second_ref, out_ref):
    zc, pair = at[0], at[1]
    rows = []
    for t in range(4):
        start = pl.multiple_of(128 * lax.rem(zc + t, 4) + 32 * pair, 32)
        rows += [first_ref[pl.ds(start, 32), :], second_ref[pl.ds(start, 32), :]]
    rows = jnp.concatenate(rows, axis=0)
    at_k = lax.broadcasted_iota(jnp.int32, (512, 512), 0)
    m = lax.broadcasted_iota(jnp.int32, (512, 512), 1)
    s, flip, low = m // 128, (m // 32) % 4, m % 32
    block = 128 * lax.rem(zc + 4 - s, 4) + 32 * jnp.bitwise_xor(pair, flip)
    pick = jnp.where(at_k == block + low, 1.0, 0.0).astype(BF16)
    out_ref[...] = jnp.dot(rows, pick, preferred_element_type=F32).astype(BF16)


def operator_rows(at, first, second):
    whole = pl.BlockSpec(memory_space=pltpu.VMEM)
    return pl.pallas_call(
        operator_kernel,
        in_specs=[pl.BlockSpec(memory_space=pltpu.SMEM), whole, whole],
        out_specs=whole,
        out_shape=jax.ShapeDtypeStruct((256, 512), BF16),
        compiler_params=params(),
        name="operator",
    )(at, first, second)


def y_kernel(s_ref, drift_ref, first_ref, second_ref, metric_ref, out_ref, s32, g32, c32):
    s32[...] = s_ref[...].astype(F32).reshape(8 * NJ * 16, 128)
    metric = metric_ref[...]
    metric2 = metric * metric
    for z in range(0, 16, 2):
        cols = jnp.concatenate(
            [s32[pl.ds(z + h, 512, stride=16), :].astype(BF16) for h in range(2)], axis=1
        )
        grad = jnp.dot(first_ref[...], cols, preferred_element_type=F32) * metric
        curv = jnp.dot(second_ref[...], cols, preferred_element_type=F32) * metric2
        for h in range(2):
            g32[pl.ds(z + h, 512, stride=16), :] = grad[:, 128 * h : 128 * (h + 1)]
            c32[pl.ds(z + h, 512, stride=16), :] = curv[:, 128 * h : 128 * (h + 1)]
    for d in range(8):
        wind = drift_ref[NJ * d : NJ * (d + 1)]
        wind = jnp.concatenate([wind[:, :16, :], wind[:, 16:, :]], axis=-1)
        p = wind.astype(F32).reshape(1024, 128) * g32[1024 * d : 1024 * (d + 1), :]
        c = c32[1024 * d : 1024 * (d + 1), :]
        pe, ce = pow_of(p), pow_of(c)
        out_ref[d, 0:1024, :] = p * jnp.exp2(13.0 - pe)
        out_ref[d, 1024:2048, :] = c * jnp.exp2(13.0 - ce)
        out_ref[d, 2048:2056, :] = jnp.broadcast_to(pe, (8, 128))
        out_ref[d, 2056:2064, :] = jnp.broadcast_to(ce, (8, 128))


def y_terms(s, drift, first, second, metric):
    whole = pl.BlockSpec(memory_space=pltpu.VMEM)
    scratch = pltpu.VMEM((8 * NJ * 16, 128), F32)
    return pl.pallas_call(
        y_kernel,
        in_specs=[whole] * 5,
        out_specs=whole,
        out_shape=jax.ShapeDtypeStruct((8, 2064, 128), F32),
        scratch_shapes=[scratch, scratch, scratch],
        compiler_params=params(),
        name="yterms",
    )(s, drift, first, second, metric)


def z_kernel(*refs):
    a_ref, pieces, outs = refs[0], refs[1:17], refs[17:21]
    rows = a_ref[...]
    results = []
    for y in range(0, YB, 2):
        cols = [jnp.concatenate([p[y + h] for p in pieces], axis=0) for h in range(2)]
        results.append(jnp.dot(rows, jnp.concatenate(cols, axis=1), preferred_element_type=F32))
    top = jnp.abs(results[0])
    for r in results[1:]:
        top = jnp.maximum(top, jnp.abs(r))
    e = pow_of(top)
    scale = jnp.exp2(13.0 - e)
    for y in range(YB):
        value = results[y // 2][:, 128 * (y % 2) : 128 * (y % 2 + 1)] * scale
        for t in range(4):
            outs[t][0, 64 * y : 64 * (y + 1), :] = value[64 * t : 64 * (t + 1), :]
    for t in range(4):
        outs[t][0, PIECE : PIECE + 16, :] = jnp.broadcast_to(e, (16, 128))


def z_terms(rows, pieces):
    out = jax.ShapeDtypeStruct((NJ // YB, PIECE + 16, 128), F32)
    return pl.pallas_call(
        z_kernel,
        grid=(NJ // YB,),
        in_specs=[pl.BlockSpec((256, 512), lambda j: (0, 0))]
        + [pl.BlockSpec((YB, NK, 128), lambda j: (j, 0, 0))] * 16,
        out_specs=[pl.BlockSpec((1, PIECE + 16, 128), lambda j: (j, 0, 0))] * 4,
        out_shape=[out] * 4,
        compiler_params=params(),
        name="zterms",
    )(rows, *pieces)


def xy_kernel(s_ref, reg_ref, drift_ref, diff_ref, first_ref, second_ref, metric_ref, p_ref, c_ref, e_ref, out_ref):
    jb = s_ref.shape[0]
    flat = s_ref[...].reshape(jb * NK, NI)
    last = (((1,), (1,)), ((), ()))
    grad = lax.dot_general(flat, first_ref[...], last, preferred_element_type=F32)
    curv = lax.dot_general(flat, second_ref[...], last, preferred_element_type=F32)
    metric = metric_ref[...]
    diff = diff_ref[...].astype(F32).reshape(jb * NK, NI)
    total = (drift_ref[...].astype(F32).reshape(jb * NK, NI) * metric) * grad
    total = total + (diff * (metric * metric)) * curv
    total = total.reshape(jb, NK, NI)
    diff = diff.reshape(jb, NK, NI)

    def native(ref, at):
        lows, highs = [], []
        for d in range(8):
            scale = jnp.exp2(e_ref[d, at : at + 1, :] - 13.0)
            v = (ref[d] * scale).reshape(jb, 16, 128)
            lows.append(v[:, :, :64])
            highs.append(v[:, :, 64:])
        return jnp.concatenate(
            [jnp.concatenate(lows, axis=-1), jnp.concatenate(highs, axis=-1)], axis=1
        )

    total = total + (native(p_ref, 0) + diff * native(c_ref, 8))
    out_ref[...] = (-5.0 / 9.0) * reg_ref[...] + 0.5 * total


def xy_terms(scalar, reg, drift, diff, first, second, metric, y_back):
    jb = 8
    field = pl.BlockSpec((jb, NK, NI), lambda j: (j, 0, 0))
    op = pl.BlockSpec((NI, NI), lambda j: (0, 0))
    n = NJ // jb
    return pl.pallas_call(
        xy_kernel,
        grid=(n,),
        in_specs=[
            field, field, field, field, op, op,
            pl.BlockSpec((1, NI), lambda j: (0, 0)),
            pl.BlockSpec((8, jb * 16, 128), lambda j: (0, j, 0)),
            pl.BlockSpec((8, jb * 16, 128), lambda j: (0, n + j, 0)),
            pl.BlockSpec((8, 16, 128), lambda j: (0, 128, 0)),
        ],
        out_specs=field,
        out_shape=jax.ShapeDtypeStruct((NJ, NK, NI), F32),
        compiler_params=params(),
        name="xyterms",
    )(scalar, reg, drift, diff, first, second, metric, y_back, y_back, y_back)


def last_kernel(at, s_ref, part_ref, drift_ref, diff_ref, metric_ref, piece_ref, *refs):
    reg_ref, out_ref = refs[-2:]
    metric = metric_ref[...][None]
    for h in range(LB):
        rows = slice(YB * h, YB * (h + 1))
        scale = jnp.exp2(piece_ref[h, PIECE : PIECE + 1, :] - 13.0)
        value = (piece_ref[h, 0:PIECE, :] * scale).reshape(YB, 2, NK, 128)
        term = (drift_ref[rows].astype(F32) * metric) * value[:, 0]
        term = term + (diff_ref[rows].astype(F32) * (metric * metric)) * value[:, 1]
        reg = part_ref[rows] + 0.5 * term
        reg_ref[rows] = reg
        out_ref[rows] = (s_ref[rows].astype(F32) + (15.0 / 16.0) * reg).astype(BF16)


LB = 2


def last_terms(at, t, scalar, part, drift, diff, metric, piece, done):
    lanes = pl.BlockSpec((LB * YB, NK, 128), lambda j, at: (j, 0, lax.rem(at[0] + 4 - t, 4)))
    return pl.pallas_call(
        last_kernel,
        grid_spec=pltpu.PrefetchScalarGridSpec(
            num_scalar_prefetch=1,
            grid=(NJ // (LB * YB),),
            in_specs=[lanes] * 4
            + [
                pl.BlockSpec((NK, 128), lambda j, at: (0, 0)),
                pl.BlockSpec((LB, PIECE + 16, 128), lambda j, at: (j, 0, 0)),
            ]
            + [pl.BlockSpec(memory_space=pl.ANY)] * len(done),
            out_specs=[lanes, lanes],
        ),
        out_shape=[
            jax.ShapeDtypeStruct((NJ, NK, NI), F32),
            jax.ShapeDtypeStruct((NJ, NK, NI), BF16),
        ],
        input_output_aliases={7 + i: i for i in range(len(done))},
        compiler_params=params(),
        name="last",
    )(at, scalar, part, drift, diff, metric, piece, *done)


def ring(x, shift):
    return lax.ppermute(x, "col", [(c, (c + 4 * shift) % 16) for c in range(16)])


def flip(x, bits):
    return lax.ppermute(x, "col", [(c, c ^ bits) for c in range(16)])


def on_device(
    scalar,
    register_in,
    drift_x,
    drift_y,
    drift_z,
    diffusivity,
    metric_x,
    metric_y,
    metric_z,
    first_x,
    second_x,
    first_y,
    second_y,
    first_z,
    second_z,
):
    col = lax.axis_index("col")
    at = jnp.stack([col // 4, col % 4]).astype(jnp.int32)
    row_send, *mine = pack(at, scalar)
    here = [mine[0]] + [ring(mine[s], s) for s in range(1, 4)]
    across = [flip(part, 2) for part in here]
    scalar_y = lax.all_to_all(row_send, "row", 0, 0, tiled=False)
    rows = operator_rows(at, first_z, second_z)
    scalar_y, rows, *early = lax.optimization_barrier([scalar_y, rows, across[0], *here[1:]])
    y_out = y_terms(scalar_y, drift_y, first_y, second_y, metric_y[:, None]).astype(F16)
    beside = [flip(part, 1) for part in here]
    y_out, *held = lax.optimization_barrier([y_out, *across, *beside])
    pieces = []
    for s in range(4):
        pieces += [here[s], held[4 + s], held[s], flip(held[s], 1)]
    y_back = lax.all_to_all(y_out, "row", 0, 0, tiled=False).astype(F32)
    z_out = z_terms(rows, pieces)
    z_back = [z_out[0]] + [ring(z_out[t].astype(F16), t).astype(F32) for t in range(1, 4)]
    part = xy_terms(
        scalar, register_in, drift_x, diffusivity, first_x, second_x, metric_x[None, :], y_back
    )
    own = lax.dynamic_slice(metric_z, (NK * col,), (NK,))
    own = jnp.broadcast_to(own[:, None], (NK, 128))
    done = ()
    for t in (0, 1, 3, 2):
        done = last_terms(at, t, scalar, part, drift_z, diffusivity, own, z_back[t], done)
    return tuple(done)


def solution(mesh):
    in_specs = (
        P("row", "col", None),
        P("row", "col", None),
        P("row", "col", None),
        P(None, "col", "row"),
        P("row", "col", None),
        P("row", "col", None),
        P(),
        P(),
        P(),
        P(),
        P(),
        P(),
        P(),
        P(),
        P(),
    )
    out_specs = (P("row", "col", None), P("row", "col", None))
    return jax.shard_map(
        on_device, mesh=mesh, in_specs=in_specs, out_specs=out_specs, check_vma=False
    )
```

```python
import jax
import jax.numpy as jnp
from jax import lax
from jax.experimental import pallas as pl
from jax.experimental.pallas import tpu as pltpu
from jax.sharding import PartitionSpec as P

F32 = jnp.float32
BF16 = jnp.bfloat16
F16 = jnp.float16

NJ, NK, NI = 64, 32, 512
YB = 16
PIECE = YB * 64
HALVES = 2
HJ = NJ // HALVES
CHUNKS = 1
CJ = NJ // CHUNKS


def params(mib):
    return pltpu.CompilerParams(vmem_limit_bytes=mib * 1024 * 1024)


def pow_of(values):
    top = jnp.max(jnp.abs(values), axis=0, keepdims=True)
    top = jnp.max(top, axis=1, keepdims=True)
    return jnp.floor(jnp.log2(jnp.maximum(top, 1e-30)))


def cut_kernel(at, s_ref, *outs):
    for s, out in enumerate(outs):
        off = pl.multiple_of(lax.rem(at[0] + s, 4) * 128, 128)
        out[...] = s_ref[:, :, pl.ds(off, 128)]


def cut(at, scalar):
    jb = 16
    return pl.pallas_call(
        cut_kernel,
        grid_spec=pltpu.PrefetchScalarGridSpec(
            num_scalar_prefetch=1,
            grid=(NJ // jb,),
            in_specs=[pl.BlockSpec((jb, NK, NI), lambda j, at: (j, 0, 0))],
            out_specs=[pl.BlockSpec((jb, NK, 128), lambda j, at: (j, 0, 0))] * 4,
        ),
        out_shape=[jax.ShapeDtypeStruct((NJ, NK, 128), BF16)] * 4,
        compiler_params=params(8),
        name="cut",
    )(at, scalar)


def pack_kernel(s_ref, after_ref, row_ref):
    for c in range(4):
        chunk = s_ref[:, :, 128 * c : 128 * (c + 1)]
        top, bot = chunk[:, :16, :], chunk[:, 16:, :]
        row_ref[2 * c] = jnp.concatenate([top[:, :, :64], bot[:, :, :64]], axis=-1)
        row_ref[2 * c + 1] = jnp.concatenate([bot[:, :, 64:], top[:, :, 64:]], axis=-1)


def merge_kernel(r1, r2, r3, *outs):
    for h, out in enumerate(outs):
        for s, r in enumerate((r1, r2, r3)):
            out[s] = r[CJ * h : CJ * (h + 1)]


def merge(parts):
    whole = pl.BlockSpec(memory_space=pltpu.VMEM)
    return pl.pallas_call(
        merge_kernel,
        in_specs=[whole] * 3,
        out_specs=[whole] * CHUNKS,
        out_shape=[jax.ShapeDtypeStruct((3, CJ, NK, 128), BF16)] * CHUNKS,
        compiler_params=params(8),
        name="merge",
    )(*parts)


def pack(scalar, after):
    jb = 16
    return pl.pallas_call(
        pack_kernel,
        grid=(NJ // jb,),
        in_specs=[
            pl.BlockSpec((jb, NK, NI), lambda j: (j, 0, 0)),
            pl.BlockSpec(memory_space=pl.ANY),
        ],
        out_specs=pl.BlockSpec((8, jb, 16, 128), lambda j: (0, j, 0, 0)),
        out_shape=jax.ShapeDtypeStruct((8, NJ, 16, 128), BF16),
        compiler_params=params(8),
        name="pack",
    )(scalar, after)


def operator_kernel(at, first_ref, second_ref, out_ref):
    zc, pair = at[0], at[1]
    rows = []
    for t in range(4):
        start = pl.multiple_of(128 * lax.rem(zc + t, 4) + 32 * pair, 32)
        rows += [first_ref[pl.ds(start, 32), :], second_ref[pl.ds(start, 32), :]]
    rows = jnp.concatenate(rows, axis=0)
    at_k = lax.broadcasted_iota(jnp.int32, (512, 512), 0)
    m = lax.broadcasted_iota(jnp.int32, (512, 512), 1)
    s, flip, low = m // 128, (m // 32) % 4, m % 32
    block = 128 * lax.rem(zc + 4 - s, 4) + 32 * jnp.bitwise_xor(pair, flip)
    pick = jnp.where(at_k == block + low, 1.0, 0.0).astype(BF16)
    out_ref[...] = jnp.dot(rows, pick, preferred_element_type=F32).astype(BF16)


def operator_rows(at, first, second):
    whole = pl.BlockSpec(memory_space=pltpu.VMEM)
    return pl.pallas_call(
        operator_kernel,
        in_specs=[pl.BlockSpec(memory_space=pltpu.SMEM), whole, whole],
        out_specs=whole,
        out_shape=jax.ShapeDtypeStruct((256, 512), BF16),
        compiler_params=params(8),
        name="operator",
    )(at, first, second)


def y_kernel(odd_ref, s_ref, drift_ref, first_ref, second_ref, metric_ref, out_ref, s32, p32, c32):
    @pl.when(pl.program_id(0) == 0)
    def _():
        s32[...] = s_ref[...].astype(F32).reshape(8 * NJ * 16, 128)
        metric = metric_ref[...]
        metric2 = metric * metric
        ops = jnp.concatenate([first_ref[...], second_ref[...]], axis=0)
        eye = lax.broadcasted_iota(jnp.int32, (512, 512), 0) == lax.broadcasted_iota(jnp.int32, (512, 512), 1)
        eye = jnp.where(eye, 1.0, 0.0).astype(BF16)
        low = 16 * odd_ref[0]
        for z in range(0, 16, 2):
            cols = jnp.concatenate(
                [s32[pl.ds(z + h, 512, stride=16), :].astype(BF16) for h in range(2)], axis=1
            )
            wind = jnp.concatenate(
                [drift_ref[z + h + at] for h in range(2) for at in (low, 16 - low)], axis=0
            )
            both = jnp.dot(ops, cols, preferred_element_type=F32)
            wind = lax.dot_general(eye, wind, (((1,), (1,)), ((), ())), preferred_element_type=F32)
            p, curv = (wind * metric) * both[:512], both[512:] * metric2
            for h in range(2):
                p32[pl.ds(z + h, 512, stride=16), :] = p[:, 128 * h : 128 * (h + 1)]
                c32[pl.ds(z + h, 512, stride=16), :] = curv[:, 128 * h : 128 * (h + 1)]

    rows = pl.ds(pl.multiple_of(pl.program_id(0) * 1024, 1024), 1024)
    p, c = p32[rows, :], c32[rows, :]
    pe, ce = pow_of(p), pow_of(c)
    out_ref[0, 0:1024, :] = p * jnp.exp2(13.0 - pe)
    out_ref[0, 1024:2048, :] = c * jnp.exp2(13.0 - ce)
    out_ref[0, 2048:2056, :] = jnp.broadcast_to(pe, (8, 128))
    out_ref[0, 2056:2064, :] = jnp.broadcast_to(ce, (8, 128))


def y_terms(odd, s, drift, first, second, metric):
    op = pl.BlockSpec((512, 512), lambda d: (0, 0))
    scratch = pltpu.VMEM((8 * NJ * 16, 128), F32)
    return pl.pallas_call(
        y_kernel,
        grid=(8,),
        in_specs=[
            pl.BlockSpec(memory_space=pltpu.SMEM),
            pl.BlockSpec((8, NJ, 16, 128), lambda d: (0, 0, 0, 0)),
            pl.BlockSpec((NK, 64, 512), lambda d: (0, 0, 0)),
            op,
            op,
            pl.BlockSpec((512, 1), lambda d: (0, 0)),
        ],
        out_specs=pl.BlockSpec((1, 2064, 128), lambda d: (d, 0, 0)),
        out_shape=jax.ShapeDtypeStruct((8, 2064, 128), F32),
        scratch_shapes=[scratch, scratch, scratch],
        compiler_params=params(40),
        name="yterms",
    )(odd, s, drift, first, second, metric)


def z_kernel(*refs):
    a_ref, firsts, rests, outs = refs[0], refs[1:5], refs[5:9], refs[9:13]
    rows = a_ref[...]
    results = []
    for y in range(0, YB, 2):
        cols = []
        for h in range(2):
            parts = [f[y + h] for f in firsts] + [m[s, y + h] for s in range(3) for m in rests]
            cols.append(jnp.concatenate(parts, axis=0))
        results.append(jnp.dot(rows, jnp.concatenate(cols, axis=1), preferred_element_type=F32))
    top = jnp.abs(results[0])
    for r in results[1:]:
        top = jnp.maximum(top, jnp.abs(r))
    e = pow_of(top)
    scale = jnp.exp2(13.0 - e)
    for y in range(YB):
        value = results[y // 2][:, 128 * (y % 2) : 128 * (y % 2 + 1)] * scale
        for t in range(4):
            outs[t][0, 64 * y : 64 * (y + 1), :] = value[64 * t : 64 * (t + 1), :]
    for t in range(4):
        outs[t][0, PIECE : PIECE + 16, :] = jnp.broadcast_to(e, (16, 128))


def z_terms(h, rows, firsts, rests):
    out = jax.ShapeDtypeStruct((HJ // YB, PIECE + 16, 128), F32)
    return pl.pallas_call(
        z_kernel,
        grid=(HJ // YB,),
        in_specs=[pl.BlockSpec((256, 512), lambda j: (0, 0))]
        + [pl.BlockSpec((YB, NK, 128), lambda j: (HJ // YB * h + j, 0, 0))] * 4
        + [pl.BlockSpec((3, YB, NK, 128), lambda j: (0, HJ // YB * h + j, 0, 0))] * 4,
        out_specs=[pl.BlockSpec((1, PIECE + 16, 128), lambda j: (j, 0, 0))] * 4,
        out_shape=[out] * 4,
        compiler_params=params(16),
        name="zterms",
    )(rows, *firsts, *rests)


def x_kernel(s_ref, reg_ref, drift_ref, diff_ref, first_ref, second_ref, metric_ref, out_ref):
    jb = s_ref.shape[0]
    flat = s_ref[...].reshape(jb * NK, NI)
    last = (((1,), (1,)), ((), ()))
    grad = lax.dot_general(flat, first_ref[...], last, preferred_element_type=F32)
    curv = lax.dot_general(flat, second_ref[...], last, preferred_element_type=F32)
    metric = metric_ref[...]
    diff = diff_ref[...].astype(F32).reshape(jb * NK, NI)
    total = (drift_ref[...].astype(F32).reshape(jb * NK, NI) * metric) * grad
    total = total + (diff * (metric * metric)) * curv
    out_ref[...] = (-5.0 / 9.0) * reg_ref[...] + 0.5 * total.reshape(jb, NK, NI)


def x_terms(scalar, reg, drift, diff, first, second, metric):
    jb = 8
    field = pl.BlockSpec((jb, NK, NI), lambda j: (j, 0, 0))
    op = pl.BlockSpec((NI, NI), lambda j: (0, 0))
    return pl.pallas_call(
        x_kernel,
        grid=(NJ // jb,),
        in_specs=[field] * 4 + [op, op, pl.BlockSpec((1, NI), lambda j: (0, 0))],
        out_specs=field,
        out_shape=jax.ShapeDtypeStruct((NJ, NK, NI), F32),
        compiler_params=params(20),
        name="xterms",
    )(scalar, reg, drift, diff, first, second, metric)


def last_kernel(at, s_ref, part_ref, drift_ref, diff_ref, metric_ref, p0, p1, p2, p3, *refs):
    reg_ref, out_ref = refs[-2:]
    metric = metric_ref[...][None]
    for t, piece in enumerate((p0, p1, p2, p3)):
        lanes = pl.ds(pl.multiple_of(lax.rem(at[0] + 4 - t, 4) * 128, 128), 128)
        scale = jnp.exp2(piece[0, PIECE : PIECE + 1, :] - 13.0)
        value = (piece[0, 0:PIECE, :] * scale).reshape(YB, 2, NK, 128)
        term = (drift_ref[:, :, lanes].astype(F32) * metric) * value[:, 0]
        term = term + (diff_ref[:, :, lanes].astype(F32) * (metric * metric)) * value[:, 1]
        reg = part_ref[:, :, lanes] + 0.5 * term
        reg_ref[:, :, lanes] = reg
        out_ref[:, :, lanes] = (s_ref[:, :, lanes].astype(F32) + (15.0 / 16.0) * reg).astype(BF16)


def last_terms(at, h, scalar, part, drift, diff, metric, pieces, done):
    n = HJ // YB
    field = pl.BlockSpec((YB, NK, NI), lambda j, at: (n * h + j, 0, 0))
    return pl.pallas_call(
        last_kernel,
        grid_spec=pltpu.PrefetchScalarGridSpec(
            num_scalar_prefetch=1,
            grid=(n,),
            in_specs=[field] * 4
            + [pl.BlockSpec((NK, 128), lambda j, at: (0, 0))]
            + [pl.BlockSpec((1, PIECE + 16, 128), lambda j, at: (j, 0, 0))] * 4
            + [pl.BlockSpec(memory_space=pl.ANY)] * len(done),
            out_specs=[field, field],
        ),
        out_shape=[
            jax.ShapeDtypeStruct((NJ, NK, NI), F32),
            jax.ShapeDtypeStruct((NJ, NK, NI), BF16),
        ],
        input_output_aliases={10 + i: i for i in range(len(done))},
        compiler_params=params(30),
        name="last",
    )(at, scalar, part, drift, diff, metric, *pieces, *done)


def add_y_kernel(part_ref, diff_ref, p_ref, c_ref, e_ref, out_ref):
    jb = part_ref.shape[0]

    low = lax.broadcasted_iota(jnp.int32, (jb, 16, 128), 2) < 64

    def native(ref, at):
        tops, bots = [], []
        for c in range(4):
            even, odd = (
                (ref[d] * jnp.exp2(e_ref[d, at : at + 1, :] - 13.0)).reshape(jb, 16, 128)
                for d in (2 * c, 2 * c + 1)
            )
            tops.append(jnp.where(low, even, odd))
            bots.append(pltpu.roll(jnp.where(low, odd, even), 64, 2))
        return jnp.concatenate(
            [jnp.concatenate(tops, axis=-1), jnp.concatenate(bots, axis=-1)], axis=1
        )

    term = native(p_ref, 0) + diff_ref[...].astype(F32) * native(c_ref, 8)
    out_ref[...] = part_ref[...] + 0.5 * term


def add_y(part, diff, y_back):
    jb = 8
    n = NJ // jb
    field = pl.BlockSpec((jb, NK, NI), lambda j: (j, 0, 0))
    return pl.pallas_call(
        add_y_kernel,
        grid=(n,),
        in_specs=[
            field,
            field,
            pl.BlockSpec((8, jb * 16, 128), lambda j: (0, j, 0)),
            pl.BlockSpec((8, jb * 16, 128), lambda j: (0, n + j, 0)),
            pl.BlockSpec((8, 16, 128), lambda j: (0, 128, 0)),
        ],
        out_specs=field,
        out_shape=jax.ShapeDtypeStruct((NJ, NK, NI), F32),
        compiler_params=params(20),
        name="addy",
    )(part, diff, y_back, y_back, y_back)


def ring(x, shift):
    return lax.ppermute(x, "col", [(c, (c + 4 * shift) % 16) for c in range(16)])


def flip(x, bits):
    return lax.ppermute(x, "col", [(c, c ^ bits) for c in range(16)])


def on_device(
    scalar,
    register_in,
    drift_x,
    drift_y,
    drift_z,
    diffusivity,
    metric_x,
    metric_y,
    metric_z,
    first_x,
    second_x,
    first_y,
    second_y,
    first_z,
    second_z,
):
    col = lax.axis_index("col")
    at = jnp.stack([col // 4, col % 4]).astype(jnp.int32)
    own = lax.dynamic_slice(metric_z, (NK * col,), (NK,))
    own = jnp.broadcast_to(own[:, None], (NK, 128))
    mine = cut(at, scalar)
    beside, across = flip(mine[0], 1), flip(mine[0], 2)
    scalar_y = lax.all_to_all(pack(scalar, beside), "row", 0, 0, tiled=False)
    rows = operator_rows(at, first_z, second_z)
    *rest, across, rows = lax.optimization_barrier(
        [ring(mine[s], s) for s in range(1, 4)] + [across, rows]
    )
    rest = merge(rest)[0]
    far = flip(rest, 2)
    scalar_y, rest = lax.optimization_barrier((scalar_y, rest))
    odd = (lax.axis_index("row") % 2).astype(jnp.int32)[None]
    wind = jnp.transpose(drift_y, (1, 2, 0))
    y_out = y_terms(odd, scalar_y, wind, first_y, second_y, metric_y[:, None]).astype(F16)
    rests = [rest, flip(rest, 1)]
    firsts = [mine[0], beside, across, flip(across, 1)]
    y_out, rests[1], firsts[3] = lax.optimization_barrier((y_out, rests[1], firsts[3]))
    y_back = lax.all_to_all(y_out, "row", 0, 0, tiled=False)
    rests += [far, flip(far, 1)]
    part = x_terms(scalar, register_in, drift_x, diffusivity, first_x, second_x, metric_x[None, :])
    z_back = []
    for h in range(HALVES):
        z_out = z_terms(h, rows, firsts, rests)
        z_back.append([z_out[0]] + [ring(z_out[t].astype(F16), t) for t in range(1, 4)])
    part = add_y(part, diffusivity, y_back.astype(F32))
    done = ()
    for h in range(HALVES):
        part, z_half, done = lax.optimization_barrier((part, z_back[h], done))
        z_half = [z.astype(F32) for z in z_half]
        done = last_terms(at, h, scalar, part, drift_z, diffusivity, own, z_half, done)
    return tuple(done)


def solution(mesh):
    in_specs = (
        P("row", "col", None),
        P("row", "col", None),
        P("row", "col", None),
        P(None, "col", "row"),
        P("row", "col", None),
        P("row", "col", None),
        P(),
        P(),
        P(),
        P(),
        P(),
        P(),
        P(),
        P(),
        P(),
    )
    out_specs = (P("row", "col", None), P("row", "col", None))
    return jax.shard_map(
        on_device, mesh=mesh, in_specs=in_specs, out_specs=out_specs, check_vma=False
    )
```

```python
import jax
import jax.numpy as jnp
from jax import lax
from jax.experimental import pallas as pl
from jax.experimental.pallas import tpu as pltpu
from jax.sharding import PartitionSpec as P

F32 = jnp.float32
BF16 = jnp.bfloat16
F16 = jnp.float16

NJ, NK, NI = 64, 32, 512
YB = 16
ZB = 20000000000
PIECE = YB * 64
HALVES = 2
HJ = NJ // HALVES
CHUNKS = 2
CJ = NJ // CHUNKS


def params(mib):
    return pltpu.CompilerParams(vmem_limit_bytes=mib * 1024 * 1024)


def pow_of(values):
    top = jnp.max(jnp.abs(values), axis=0, keepdims=True)
    top = jnp.max(top, axis=1, keepdims=True)
    return jnp.floor(jnp.log2(jnp.maximum(top, 1e-30)))


def cut_kernel(at, s_ref, *outs):
    for s, out in enumerate(outs):
        off = pl.multiple_of(lax.rem(at[0] + s, 4) * 128, 128)
        out[...] = s_ref[:, :, pl.ds(off, 128)]


def cut(at, scalar):
    jb = 16
    return pl.pallas_call(
        cut_kernel,
        grid_spec=pltpu.PrefetchScalarGridSpec(
            num_scalar_prefetch=1,
            grid=(NJ // jb,),
            in_specs=[pl.BlockSpec((jb, NK, NI), lambda j, at: (j, 0, 0))],
            out_specs=[pl.BlockSpec((jb, NK, 128), lambda j, at: (j, 0, 0))] * 4,
        ),
        out_shape=[jax.ShapeDtypeStruct((NJ, NK, 128), BF16)] * 4,
        compiler_params=params(8),
        name="cut",
    )(at, scalar)


def pack_kernel(s_ref, after_ref, row_ref):
    for c in range(4):
        chunk = s_ref[:, :, 128 * c : 128 * (c + 1)]
        top, bot = chunk[:, :16, :], chunk[:, 16:, :]
        row_ref[2 * c] = jnp.concatenate([top[:, :, :64], bot[:, :, :64]], axis=-1)
        row_ref[2 * c + 1] = jnp.concatenate([bot[:, :, 64:], top[:, :, 64:]], axis=-1)


def merge_kernel(r1, r2, r3, *outs):
    for h, out in enumerate(outs):
        for s, r in enumerate((r1, r2, r3)):
            out[s] = r[CJ * h : CJ * (h + 1)]


def merge(parts):
    whole = pl.BlockSpec(memory_space=pltpu.VMEM)
    return pl.pallas_call(
        merge_kernel,
        in_specs=[whole] * 3,
        out_specs=[whole] * CHUNKS,
        out_shape=[jax.ShapeDtypeStruct((3, CJ, NK, 128), BF16)] * CHUNKS,
        compiler_params=params(8),
        cost_estimate=pl.CostEstimate(flops=20 * 10**9, transcendentals=0, bytes_accessed=3 << 20),
        name="merge",
    )(*parts)


def pack(scalar, after):
    jb = 16
    return pl.pallas_call(
        pack_kernel,
        grid=(NJ // jb,),
        in_specs=[
            pl.BlockSpec((jb, NK, NI), lambda j: (j, 0, 0)),
            pl.BlockSpec(memory_space=pl.ANY),
        ],
        out_specs=pl.BlockSpec((8, jb, 16, 128), lambda j: (0, j, 0, 0)),
        out_shape=jax.ShapeDtypeStruct((8, NJ, 16, 128), BF16),
        compiler_params=params(8),
        name="pack",
    )(scalar, after)


def operator_kernel(at, first_ref, second_ref, first_y, second_y, drift_ref, out_ref, ops_ref, wind_ref):
    zc, pair = at[0], at[1]
    rows = []
    for t in range(4):
        start = pl.multiple_of(128 * lax.rem(zc + t, 4) + 32 * pair, 32)
        rows += [first_ref[pl.ds(start, 32), :], second_ref[pl.ds(start, 32), :]]
    rows = jnp.concatenate(rows, axis=0)
    at_k = lax.broadcasted_iota(jnp.int32, (512, 512), 0)
    m = lax.broadcasted_iota(jnp.int32, (512, 512), 1)
    s, flip, low = m // 128, (m // 32) % 4, m % 32
    block = 128 * lax.rem(zc + 4 - s, 4) + 32 * jnp.bitwise_xor(pair, flip)
    pick = jnp.where(at_k == block + low, 1.0, 0.0).astype(BF16)
    out_ref[...] = jnp.dot(rows, pick, preferred_element_type=F32).astype(BF16)
    ops_ref[0:512] = first_y[...]
    ops_ref[512:1024] = second_y[...]
    wind_ref[...] = drift_ref[...]


def operator_rows(at, first, second, first_y, second_y, drift):
    whole = pl.BlockSpec(memory_space=pltpu.VMEM)
    return pl.pallas_call(
        operator_kernel,
        in_specs=[pl.BlockSpec(memory_space=pltpu.SMEM)] + [whole] * 5,
        out_specs=[whole] * 3,
        out_shape=[
            jax.ShapeDtypeStruct((256, 512), BF16),
            jax.ShapeDtypeStruct((1024, 512), BF16),
            jax.ShapeDtypeStruct((NK, 64, 512), BF16),
        ],
        compiler_params=params(16),
        name="operator",
    )(at, first, second, first_y, second_y, drift)


def y_kernel(odd_ref, s_ref, drift_ref, ops_ref, metric_ref, out_ref, s32, p32, c32):
    @pl.when(pl.program_id(0) == 0)
    def _():
        s32[...] = s_ref[...].astype(F32).reshape(8 * NJ * 16, 128)
        metric = metric_ref[...]
        metric2 = metric * metric
        ops = ops_ref[...]
        eye = lax.broadcasted_iota(jnp.int32, (512, 512), 0) == lax.broadcasted_iota(jnp.int32, (512, 512), 1)
        eye = jnp.where(eye, 1.0, 0.0).astype(BF16)
        low = 16 * odd_ref[0]
        for z in range(0, 16, 2):
            cols = jnp.concatenate(
                [s32[pl.ds(z + h, 512, stride=16), :].astype(BF16) for h in range(2)], axis=1
            )
            wind = jnp.concatenate(
                [drift_ref[z + h + at] for h in range(2) for at in (low, 16 - low)], axis=0
            )
            both = jnp.dot(ops, cols, preferred_element_type=F32)
            wind = lax.dot_general(eye, wind, (((1,), (1,)), ((), ())), preferred_element_type=F32)
            p, curv = (wind * metric) * both[:512], both[512:] * metric2
            for h in range(2):
                p32[pl.ds(z + h, 512, stride=16), :] = p[:, 128 * h : 128 * (h + 1)]
                c32[pl.ds(z + h, 512, stride=16), :] = curv[:, 128 * h : 128 * (h + 1)]

    rows = pl.ds(pl.multiple_of(pl.program_id(0) * 1024, 1024), 1024)
    p, c = p32[rows, :], c32[rows, :]
    pe, ce = pow_of(p), pow_of(c)
    out_ref[0, 0:1024, :] = p * jnp.exp2(13.0 - pe)
    out_ref[0, 1024:2048, :] = c * jnp.exp2(13.0 - ce)
    out_ref[0, 2048:2056, :] = jnp.broadcast_to(pe, (8, 128))
    out_ref[0, 2056:2064, :] = jnp.broadcast_to(ce, (8, 128))


def y_terms(odd, s, drift, ops, metric):
    scratch = pltpu.VMEM((8 * NJ * 16, 128), F32)
    return pl.pallas_call(
        y_kernel,
        grid=(8,),
        in_specs=[
            pl.BlockSpec(memory_space=pltpu.SMEM),
            pl.BlockSpec((8, NJ, 16, 128), lambda d: (0, 0, 0, 0)),
            pl.BlockSpec((NK, 64, 512), lambda d: (0, 0, 0)),
            pl.BlockSpec((1024, 512), lambda d: (0, 0)),
            pl.BlockSpec((512, 1), lambda d: (0, 0)),
        ],
        out_specs=pl.BlockSpec((1, 2064, 128), lambda d: (d, 0, 0)),
        out_shape=jax.ShapeDtypeStruct((8, 2064, 128), F32),
        scratch_shapes=[scratch, scratch, scratch],
        compiler_params=params(40),
        cost_estimate=pl.CostEstimate(flops=1000, transcendentals=0, bytes_accessed=8 << 10),
        name="yterms",
    )(odd, s, drift, ops, metric)


def z_kernel(*refs):
    a_ref, firsts, rests, outs = refs[0], refs[1:5], refs[5:9], refs[9:13]
    rows = a_ref[...]
    results = []
    for y in range(0, YB, 2):
        cols = []
        for h in range(2):
            parts = [f[y + h] for f in firsts] + [m[s, y + h] for s in range(3) for m in rests]
            cols.append(jnp.concatenate(parts, axis=0))
        results.append(jnp.dot(rows, jnp.concatenate(cols, axis=1), preferred_element_type=F32))
    top = jnp.abs(results[0])
    for r in results[1:]:
        top = jnp.maximum(top, jnp.abs(r))
    e = pow_of(top)
    scale = jnp.exp2(13.0 - e)
    for y in range(YB):
        value = results[y // 2][:, 128 * (y % 2) : 128 * (y % 2 + 1)] * scale
        for t in range(4):
            outs[t][0, 64 * y : 64 * (y + 1), :] = value[64 * t : 64 * (t + 1), :]
    for t in range(4):
        outs[t][0, PIECE : PIECE + 16, :] = jnp.broadcast_to(e, (16, 128))


def z_terms(h, rows, firsts, rests):
    out = jax.ShapeDtypeStruct((HJ // YB, PIECE + 16, 128), F32)
    return pl.pallas_call(
        z_kernel,
        grid=(HJ // YB,),
        in_specs=[pl.BlockSpec((256, 512), lambda j: (0, 0))]
        + [pl.BlockSpec((YB, NK, 128), lambda j: (HJ // YB * h + j, 0, 0))] * 4
        + [pl.BlockSpec((3, YB, NK, 128), lambda j: (0, j, 0, 0))] * 4,
        out_specs=[pl.BlockSpec((1, PIECE + 16, 128), lambda j: (j, 0, 0))] * 4,
        out_shape=[out] * 4,
        compiler_params=params(16),
        cost_estimate=pl.CostEstimate(flops=(1000, ZB)[h], transcendentals=0, bytes_accessed=8 << 10),
        name="zterms",
    )(rows, *firsts, *rests)


def x_kernel(s_ref, reg_ref, drift_ref, diff_ref, first_ref, second_ref, metric_ref, out_ref):
    jb = s_ref.shape[0]
    flat = s_ref[...].reshape(jb * NK, NI)
    last = (((1,), (1,)), ((), ()))
    grad = lax.dot_general(flat, first_ref[...], last, preferred_element_type=F32)
    curv = lax.dot_general(flat, second_ref[...], last, preferred_element_type=F32)
    metric = metric_ref[...]
    diff = diff_ref[...].astype(F32).reshape(jb * NK, NI)
    total = (drift_ref[...].astype(F32).reshape(jb * NK, NI) * metric) * grad
    total = total + (diff * (metric * metric)) * curv
    out_ref[...] = (-5.0 / 9.0) * reg_ref[...] + 0.5 * total.reshape(jb, NK, NI)


def x_terms(scalar, reg, drift, diff, first, second, metric):
    jb = 8
    field = pl.BlockSpec((jb, NK, NI), lambda j: (j, 0, 0))
    op = pl.BlockSpec((NI, NI), lambda j: (0, 0))
    return pl.pallas_call(
        x_kernel,
        grid=(NJ // jb,),
        in_specs=[field] * 4 + [op, op, pl.BlockSpec((1, NI), lambda j: (0, 0))],
        out_specs=field,
        out_shape=jax.ShapeDtypeStruct((NJ, NK, NI), F32),
        compiler_params=params(20),
        cost_estimate=pl.CostEstimate(flops=1000, transcendentals=0, bytes_accessed=8 << 10),
        name="xterms",
    )(scalar, reg, drift, diff, first, second, metric)


def last_kernel(at, s_ref, part_ref, drift_ref, diff_ref, metric_ref, p0, p1, p2, p3, *refs):
    reg_ref, out_ref = refs[-2:]
    metric = metric_ref[...][None]
    for t, piece in enumerate((p0, p1, p2, p3)):
        lanes = pl.ds(pl.multiple_of(lax.rem(at[0] + 4 - t, 4) * 128, 128), 128)
        scale = jnp.exp2(piece[0, PIECE : PIECE + 1, :] - 13.0)
        value = (piece[0, 0:PIECE, :] * scale).reshape(YB, 2, NK, 128)
        term = (drift_ref[:, :, lanes].astype(F32) * metric) * value[:, 0]
        term = term + (diff_ref[:, :, lanes].astype(F32) * (metric * metric)) * value[:, 1]
        reg = part_ref[:, :, lanes] + 0.5 * term
        reg_ref[:, :, lanes] = reg
        out_ref[:, :, lanes] = (s_ref[:, :, lanes].astype(F32) + (15.0 / 16.0) * reg).astype(BF16)


def last_terms(at, h, scalar, part, drift, diff, metric, pieces, done):
    n = HJ // YB
    field = pl.BlockSpec((YB, NK, NI), lambda j, at: (n * h + j, 0, 0))
    return pl.pallas_call(
        last_kernel,
        grid_spec=pltpu.PrefetchScalarGridSpec(
            num_scalar_prefetch=1,
            grid=(n,),
            in_specs=[field] * 4
            + [pl.BlockSpec((NK, 128), lambda j, at: (0, 0))]
            + [pl.BlockSpec((1, PIECE + 16, 128), lambda j, at: (j, 0, 0))] * 4
            + [pl.BlockSpec(memory_space=pl.ANY)] * len(done),
            out_specs=[field, field],
        ),
        out_shape=[
            jax.ShapeDtypeStruct((NJ, NK, NI), F32),
            jax.ShapeDtypeStruct((NJ, NK, NI), BF16),
        ],
        input_output_aliases={10 + i: i for i in range(len(done))},
        compiler_params=params(30),
        name="last",
    )(at, scalar, part, drift, diff, metric, *pieces, *done)


def add_y_kernel(part_ref, diff_ref, p_ref, c_ref, e_ref, out_ref):
    jb = part_ref.shape[0]

    low = lax.broadcasted_iota(jnp.int32, (jb, 16, 128), 2) < 64

    def native(ref, at):
        tops, bots = [], []
        for c in range(4):
            even, odd = (
                (ref[d] * jnp.exp2(e_ref[d, at : at + 1, :] - 13.0)).reshape(jb, 16, 128)
                for d in (2 * c, 2 * c + 1)
            )
            tops.append(jnp.where(low, even, odd))
            bots.append(pltpu.roll(jnp.where(low, odd, even), 64, 2))
        return jnp.concatenate(
            [jnp.concatenate(tops, axis=-1), jnp.concatenate(bots, axis=-1)], axis=1
        )

    term = native(p_ref, 0) + diff_ref[...].astype(F32) * native(c_ref, 8)
    out_ref[...] = part_ref[...] + 0.5 * term


def add_y(part, diff, y_back):
    jb = 8
    n = NJ // jb
    field = pl.BlockSpec((jb, NK, NI), lambda j: (j, 0, 0))
    return pl.pallas_call(
        add_y_kernel,
        grid=(n,),
        in_specs=[
            field,
            field,
            pl.BlockSpec((8, jb * 16, 128), lambda j: (0, j, 0)),
            pl.BlockSpec((8, jb * 16, 128), lambda j: (0, n + j, 0)),
            pl.BlockSpec((8, 16, 128), lambda j: (0, 128, 0)),
        ],
        out_specs=field,
        out_shape=jax.ShapeDtypeStruct((NJ, NK, NI), F32),
        compiler_params=params(20),
        name="addy",
    )(part, diff, y_back, y_back, y_back)


def ring(x, shift):
    return lax.ppermute(x, "col", [(c, (c + 4 * shift) % 16) for c in range(16)])


def flip(x, bits):
    return lax.ppermute(x, "col", [(c, c ^ bits) for c in range(16)])


def on_device(
    scalar,
    register_in,
    drift_x,
    drift_y,
    drift_z,
    diffusivity,
    metric_x,
    metric_y,
    metric_z,
    first_x,
    second_x,
    first_y,
    second_y,
    first_z,
    second_z,
):
    col = lax.axis_index("col")
    at = jnp.stack([col // 4, col % 4]).astype(jnp.int32)
    own = lax.dynamic_slice(metric_z, (NK * col,), (NK,))
    own = jnp.broadcast_to(own[:, None], (NK, 128))
    mine = cut(at, scalar)
    beside, across = flip(mine[0], 1), flip(mine[0], 2)
    scalar_y = lax.all_to_all(pack(scalar, mine[0]), "row", 0, 0, tiled=False)
    wind = jnp.transpose(drift_y, (1, 2, 0))
    rows, ops, wind = operator_rows(at, first_z, second_z, first_y, second_y, wind)
    part = x_terms(scalar, register_in, drift_x, diffusivity, first_x, second_x, metric_x[None, :])
    *rest, across, rows, ops, wind, part = lax.optimization_barrier(
        [ring(mine[s], s) for s in range(1, 4)] + [across, rows, ops, wind, part]
    )
    rest = list(merge(rest))
    far = [flip(rest[0], 2)]
    near = [flip(part, 1) for part in rest]
    scalar_y, *rest = lax.optimization_barrier((scalar_y, *rest))
    odd = (lax.axis_index("row") % 2).astype(jnp.int32)[None]
    y_out = y_terms(odd, scalar_y, wind, ops, metric_y[:, None]).astype(F16)
    far[0], rest[1] = lax.optimization_barrier((far[0], rest[1]))
    far.append(flip(rest[1], 2))
    near[0], across, far[0], y_out = lax.optimization_barrier((near[0], across, far[0], y_out))
    firsts = [mine[0], beside, across, flip(across, 1)]

    def z_half(h):
        z_out = z_terms(h, rows, firsts, [rest[h], near[h], far[h], flip(far[h], 1)])
        return [z_out[0]] + [z_out[t].astype(F16) for t in range(1, 4)]

    def send_back(z_out):
        return [z_out[0]] + [ring(z_out[t], t) for t in range(1, 4)]

    z_send = z_half(0)
    y_out, z_send = lax.optimization_barrier((y_out, z_send))
    z_back = [send_back(z_send)]
    y_back = lax.all_to_all(y_out, "row", 0, 0, tiled=False)
    z_back.append(send_back(z_half(1)))
    part = add_y(part, diffusivity, y_back.astype(F32))
    z_back[0] = [z.astype(F32) for z in z_back[0]]
    part, z_back[1] = lax.optimization_barrier((part, z_back[1]))
    z_back[1] = [z.astype(F32) for z in z_back[1]]
    done = ()
    for h in range(HALVES):
        done = last_terms(at, h, scalar, part, drift_z, diffusivity, own, z_back[h], done)
    return tuple(done)


def solution(mesh):
    in_specs = (
        P("row", "col", None),
        P("row", "col", None),
        P("row", "col", None),
        P(None, "col", "row"),
        P("row", "col", None),
        P("row", "col", None),
        P(),
        P(),
        P(),
        P(),
        P(),
        P(),
        P(),
        P(),
        P(),
    )
    out_specs = (P("row", "col", None), P("row", "col", None))
    return jax.shard_map(
        on_device, mesh=mesh, in_specs=in_specs, out_specs=out_specs, check_vma=False
    )
```

```python
import jax
import jax.numpy as jnp
from jax import lax
from jax.experimental import pallas as pl
from jax.experimental.pallas import tpu as pltpu
from jax.sharding import PartitionSpec as P

F32 = jnp.float32
BF16 = jnp.bfloat16
F16 = jnp.float16

NJ, NK, NI = 64, 32, 512
YB = 16
ZB = 20000000000
PIECE = YB * 64
HALVES = 2
HJ = NJ // HALVES
CHUNKS = 2
CJ = NJ // CHUNKS


def params(mib):
    return pltpu.CompilerParams(vmem_limit_bytes=mib * 1024 * 1024)


def pow_of(values):
    top = jnp.max(jnp.abs(values), axis=0, keepdims=True)
    top = jnp.max(top, axis=1, keepdims=True)
    return jnp.floor(jnp.log2(jnp.maximum(top, 1e-30)))


def cut_kernel(at, s_ref, *outs):
    for s, out in enumerate(outs):
        off = pl.multiple_of(lax.rem(at[0] + s, 4) * 128, 128)
        out[...] = s_ref[:, :, pl.ds(off, 128)]


def cut(at, scalar):
    jb = 16
    return pl.pallas_call(
        cut_kernel,
        grid_spec=pltpu.PrefetchScalarGridSpec(
            num_scalar_prefetch=1,
            grid=(NJ // jb,),
            in_specs=[pl.BlockSpec((jb, NK, NI), lambda j, at: (j, 0, 0))],
            out_specs=[pl.BlockSpec((jb, NK, 128), lambda j, at: (j, 0, 0))] * 4,
        ),
        out_shape=[jax.ShapeDtypeStruct((NJ, NK, 128), BF16)] * 4,
        compiler_params=params(8),
        name="cut",
    )(at, scalar)


def pack_kernel(s_ref, after_ref, row_ref):
    for c in range(4):
        chunk = s_ref[:, :, 128 * c : 128 * (c + 1)]
        top, bot = chunk[:, :16, :], chunk[:, 16:, :]
        row_ref[2 * c] = jnp.concatenate([top[:, :, :64], bot[:, :, :64]], axis=-1)
        row_ref[2 * c + 1] = jnp.concatenate([bot[:, :, 64:], top[:, :, 64:]], axis=-1)


def merge_kernel(r1, r2, r3, *outs):
    for h, out in enumerate(outs):
        for s, r in enumerate((r1, r2, r3)):
            out[s] = r[CJ * h : CJ * (h + 1)]


def merge(parts):
    whole = pl.BlockSpec(memory_space=pltpu.VMEM)
    return pl.pallas_call(
        merge_kernel,
        in_specs=[whole] * 3,
        out_specs=[whole] * CHUNKS,
        out_shape=[jax.ShapeDtypeStruct((3, CJ, NK, 128), BF16)] * CHUNKS,
        compiler_params=params(8),
        cost_estimate=pl.CostEstimate(flops=20 * 10**9, transcendentals=0, bytes_accessed=3 << 20),
        name="merge",
    )(*parts)


def pack(scalar, after):
    jb = 16
    return pl.pallas_call(
        pack_kernel,
        grid=(NJ // jb,),
        in_specs=[
            pl.BlockSpec((jb, NK, NI), lambda j: (j, 0, 0)),
            pl.BlockSpec(memory_space=pl.ANY),
        ],
        out_specs=pl.BlockSpec((8, jb, 16, 128), lambda j: (0, j, 0, 0)),
        out_shape=jax.ShapeDtypeStruct((8, NJ, 16, 128), BF16),
        compiler_params=params(8),
        name="pack",
    )(scalar, after)


def operator_kernel(at, first_ref, second_ref, first_y, second_y, drift_ref, out_ref, ops_ref, wind_ref):
    zc, pair = at[0], at[1]
    rows = []
    for t in range(4):
        start = pl.multiple_of(128 * lax.rem(zc + t, 4) + 32 * pair, 32)
        rows += [first_ref[pl.ds(start, 32), :], second_ref[pl.ds(start, 32), :]]
    rows = jnp.concatenate(rows, axis=0)
    at_k = lax.broadcasted_iota(jnp.int32, (512, 512), 0)
    m = lax.broadcasted_iota(jnp.int32, (512, 512), 1)
    s, flip, low = m // 128, (m // 32) % 4, m % 32
    block = 128 * lax.rem(zc + 4 - s, 4) + 32 * jnp.bitwise_xor(pair, flip)
    pick = jnp.where(at_k == block + low, 1.0, 0.0).astype(BF16)
    out_ref[...] = jnp.dot(rows, pick, preferred_element_type=F32).astype(BF16)
    ops_ref[0:512] = first_y[...]
    ops_ref[512:1024] = second_y[...]
    wind_ref[...] = drift_ref[...]


def operator_rows(at, first, second, first_y, second_y, drift):
    whole = pl.BlockSpec(memory_space=pltpu.VMEM)
    return pl.pallas_call(
        operator_kernel,
        in_specs=[pl.BlockSpec(memory_space=pltpu.SMEM)] + [whole] * 5,
        out_specs=[whole] * 3,
        out_shape=[
            jax.ShapeDtypeStruct((256, 512), BF16),
            jax.ShapeDtypeStruct((1024, 512), BF16),
            jax.ShapeDtypeStruct((NK, 64, 512), BF16),
        ],
        compiler_params=params(16),
        name="operator",
    )(at, first, second, first_y, second_y, drift)


def y_kernel(odd_ref, s_ref, drift_ref, ops_ref, metric_ref, out_ref, s32, p32, c32):
    @pl.when(pl.program_id(0) == 0)
    def _():
        s32[...] = s_ref[...].astype(F32).reshape(8 * NJ * 16, 128)
        metric = metric_ref[...]
        metric2 = metric * metric
        ops = ops_ref[...]
        eye = lax.broadcasted_iota(jnp.int32, (512, 512), 0) == lax.broadcasted_iota(jnp.int32, (512, 512), 1)
        eye = jnp.where(eye, 1.0, 0.0).astype(BF16)
        low = 16 * odd_ref[0]
        for z in range(0, 16, 2):
            cols = jnp.concatenate(
                [s32[pl.ds(z + h, 512, stride=16), :].astype(BF16) for h in range(2)], axis=1
            )
            wind = jnp.concatenate(
                [drift_ref[z + h + at] for h in range(2) for at in (low, 16 - low)], axis=0
            )
            both = jnp.dot(ops, cols, preferred_element_type=F32)
            wind = lax.dot_general(eye, wind, (((1,), (1,)), ((), ())), preferred_element_type=F32)
            p, curv = (wind * metric) * both[:512], both[512:] * metric2
            for h in range(2):
                p32[pl.ds(z + h, 512, stride=16), :] = p[:, 128 * h : 128 * (h + 1)]
                c32[pl.ds(z + h, 512, stride=16), :] = curv[:, 128 * h : 128 * (h + 1)]

    rows = pl.ds(pl.multiple_of(pl.program_id(0) * 1024, 1024), 1024)
    p, c = p32[rows, :], c32[rows, :]
    pe, ce = pow_of(p), pow_of(c)
    out_ref[0, 0:1024, :] = p * jnp.exp2(13.0 - pe)
    out_ref[0, 1024:2048, :] = c * jnp.exp2(13.0 - ce)
    out_ref[0, 2048:2056, :] = jnp.broadcast_to(pe, (8, 128))
    out_ref[0, 2056:2064, :] = jnp.broadcast_to(ce, (8, 128))


def y_terms(odd, s, drift, ops, metric):
    scratch = pltpu.VMEM((8 * NJ * 16, 128), F32)
    return pl.pallas_call(
        y_kernel,
        grid=(8,),
        in_specs=[
            pl.BlockSpec(memory_space=pltpu.SMEM),
            pl.BlockSpec((8, NJ, 16, 128), lambda d: (0, 0, 0, 0)),
            pl.BlockSpec((NK, 64, 512), lambda d: (0, 0, 0)),
            pl.BlockSpec((1024, 512), lambda d: (0, 0)),
            pl.BlockSpec((512, 1), lambda d: (0, 0)),
        ],
        out_specs=pl.BlockSpec((1, 2064, 128), lambda d: (d, 0, 0)),
        out_shape=jax.ShapeDtypeStruct((8, 2064, 128), F32),
        scratch_shapes=[scratch, scratch, scratch],
        compiler_params=params(40),
        cost_estimate=pl.CostEstimate(flops=1000, transcendentals=0, bytes_accessed=8 << 10),
        name="yterms",
    )(odd, s, drift, ops, metric)


def z_kernel(*refs):
    a_ref, firsts, rests, outs = refs[0], refs[1:5], refs[5:9], refs[9:13]
    rows = a_ref[...]
    results = []
    for y in range(0, YB, 2):
        cols = []
        for h in range(2):
            parts = [f[y + h] for f in firsts] + [m[s, y + h] for s in range(3) for m in rests]
            cols.append(jnp.concatenate(parts, axis=0))
        results.append(jnp.dot(rows, jnp.concatenate(cols, axis=1), preferred_element_type=F32))
    top = jnp.abs(results[0])
    for r in results[1:]:
        top = jnp.maximum(top, jnp.abs(r))
    e = pow_of(top)
    scale = jnp.exp2(13.0 - e)
    for y in range(YB):
        value = results[y // 2][:, 128 * (y % 2) : 128 * (y % 2 + 1)] * scale
        for t in range(4):
            outs[t][0, 64 * y : 64 * (y + 1), :] = value[64 * t : 64 * (t + 1), :]
    for t in range(4):
        outs[t][0, PIECE : PIECE + 16, :] = jnp.broadcast_to(e, (16, 128))


def z_terms(h, rows, firsts, rests):
    out = jax.ShapeDtypeStruct((HJ // YB, PIECE + 16, 128), F32)
    return pl.pallas_call(
        z_kernel,
        grid=(HJ // YB,),
        in_specs=[pl.BlockSpec((256, 512), lambda j: (0, 0))]
        + [pl.BlockSpec((YB, NK, 128), lambda j: (HJ // YB * h + j, 0, 0))] * 4
        + [pl.BlockSpec((3, YB, NK, 128), lambda j: (0, j, 0, 0))] * 4,
        out_specs=[pl.BlockSpec((1, PIECE + 16, 128), lambda j: (j, 0, 0))] * 4,
        out_shape=[out] * 4,
        compiler_params=params(16),
        cost_estimate=pl.CostEstimate(flops=(1000, ZB)[h], transcendentals=0, bytes_accessed=8 << 10),
        name="zterms",
    )(rows, *firsts, *rests)


def x_kernel(s_ref, reg_ref, drift_ref, diff_ref, first_ref, second_ref, metric_ref, out_ref):
    jb = s_ref.shape[0]
    flat = s_ref[...].reshape(jb * NK, NI)
    last = (((1,), (1,)), ((), ()))
    grad = lax.dot_general(flat, first_ref[...], last, preferred_element_type=F32)
    curv = lax.dot_general(flat, second_ref[...], last, preferred_element_type=F32)
    metric = metric_ref[...]
    diff = diff_ref[...].astype(F32).reshape(jb * NK, NI)
    total = (drift_ref[...].astype(F32).reshape(jb * NK, NI) * metric) * grad
    total = total + (diff * (metric * metric)) * curv
    out_ref[...] = (-5.0 / 9.0) * reg_ref[...] + 0.5 * total.reshape(jb, NK, NI)


def x_terms(scalar, reg, drift, diff, first, second, metric):
    jb = 8
    field = pl.BlockSpec((jb, NK, NI), lambda j: (j, 0, 0))
    op = pl.BlockSpec((NI, NI), lambda j: (0, 0))
    return pl.pallas_call(
        x_kernel,
        grid=(NJ // jb,),
        in_specs=[field] * 4 + [op, op, pl.BlockSpec((1, NI), lambda j: (0, 0))],
        out_specs=field,
        out_shape=jax.ShapeDtypeStruct((NJ, NK, NI), F32),
        compiler_params=params(20),
        cost_estimate=pl.CostEstimate(flops=1000, transcendentals=0, bytes_accessed=8 << 10),
        name="xterms",
    )(scalar, reg, drift, diff, first, second, metric)


def last_kernel(at, s_ref, part_ref, drift_ref, diff_ref, metric_ref, *refs):
    pieces, (reg_ref, out_ref) = refs[:-2], refs[-2:]
    metric = metric_ref[...][None]

    def finish(pieces):
        for t, piece in enumerate(pieces):
            lanes = pl.ds(pl.multiple_of(lax.rem(at[0] + 4 - t, 4) * 128, 128), 128)
            scale = jnp.exp2(piece[0, PIECE : PIECE + 1, :] - 13.0)
            value = (piece[0, 0:PIECE, :] * scale).reshape(YB, 2, NK, 128)
            term = (drift_ref[:, :, lanes].astype(F32) * metric) * value[:, 0]
            term = term + (diff_ref[:, :, lanes].astype(F32) * (metric * metric)) * value[:, 1]
            reg = part_ref[:, :, lanes] + 0.5 * term
            reg_ref[:, :, lanes] = reg
            out_ref[:, :, lanes] = (s_ref[:, :, lanes].astype(F32) + (15.0 / 16.0) * reg).astype(BF16)

    for h in range(HALVES):

        @pl.when(pl.program_id(0) // (HJ // YB) == h)
        def _():
            finish(pieces[4 * h : 4 * (h + 1)])


def last_terms(at, scalar, part, drift, diff, metric, pieces):
    m = HJ // YB
    field = pl.BlockSpec((YB, NK, NI), lambda j, at: (j, 0, 0))
    specs = []
    for h in range(HALVES):
        specs += [
            pl.BlockSpec((1, PIECE + 16, 128), lambda j, at, h=h: (jnp.clip(j - m * h, 0, m - 1), 0, 0))
        ] * 4
    return pl.pallas_call(
        last_kernel,
        grid_spec=pltpu.PrefetchScalarGridSpec(
            num_scalar_prefetch=1,
            grid=(NJ // YB,),
            in_specs=[field] * 4 + [pl.BlockSpec((NK, 128), lambda j, at: (0, 0))] + specs,
            out_specs=[field, field],
        ),
        out_shape=[
            jax.ShapeDtypeStruct((NJ, NK, NI), F32),
            jax.ShapeDtypeStruct((NJ, NK, NI), BF16),
        ],
        compiler_params=params(30),
        name="last",
    )(at, scalar, part, drift, diff, metric, *pieces)


def add_y_kernel(part_ref, diff_ref, p_ref, c_ref, e_ref, out_ref):
    jb = part_ref.shape[0]

    low = lax.broadcasted_iota(jnp.int32, (jb, 16, 128), 2) < 64

    def native(ref, at):
        tops, bots = [], []
        for c in range(4):
            even, odd = (
                (ref[d] * jnp.exp2(e_ref[d, at : at + 1, :] - 13.0)).reshape(jb, 16, 128)
                for d in (2 * c, 2 * c + 1)
            )
            tops.append(jnp.where(low, even, odd))
            bots.append(pltpu.roll(jnp.where(low, odd, even), 64, 2))
        return jnp.concatenate(
            [jnp.concatenate(tops, axis=-1), jnp.concatenate(bots, axis=-1)], axis=1
        )

    term = native(p_ref, 0) + diff_ref[...].astype(F32) * native(c_ref, 8)
    out_ref[...] = part_ref[...] + 0.5 * term


def add_y(part, diff, y_back):
    jb = 8
    n = NJ // jb
    field = pl.BlockSpec((jb, NK, NI), lambda j: (j, 0, 0))
    return pl.pallas_call(
        add_y_kernel,
        grid=(n,),
        in_specs=[
            field,
            field,
            pl.BlockSpec((8, jb * 16, 128), lambda j: (0, j, 0)),
            pl.BlockSpec((8, jb * 16, 128), lambda j: (0, n + j, 0)),
            pl.BlockSpec((8, 16, 128), lambda j: (0, 128, 0)),
        ],
        out_specs=field,
        out_shape=jax.ShapeDtypeStruct((NJ, NK, NI), F32),
        compiler_params=params(20),
        name="addy",
    )(part, diff, y_back, y_back, y_back)


def ring(x, shift):
    return lax.ppermute(x, "col", [(c, (c + 4 * shift) % 16) for c in range(16)])


def flip(x, bits):
    return lax.ppermute(x, "col", [(c, c ^ bits) for c in range(16)])


def on_device(
    scalar,
    register_in,
    drift_x,
    drift_y,
    drift_z,
    diffusivity,
    metric_x,
    metric_y,
    metric_z,
    first_x,
    second_x,
    first_y,
    second_y,
    first_z,
    second_z,
):
    col = lax.axis_index("col")
    at = jnp.stack([col // 4, col % 4]).astype(jnp.int32)
    own = lax.dynamic_slice(metric_z, (NK * col,), (NK,))
    own = jnp.broadcast_to(own[:, None], (NK, 128))
    mine = cut(at, scalar)
    beside, across = flip(mine[0], 1), flip(mine[0], 2)
    scalar_y = lax.all_to_all(pack(scalar, mine[0]), "row", 0, 0, tiled=False)
    wind = jnp.transpose(drift_y, (1, 2, 0))
    rows, ops, wind = operator_rows(at, first_z, second_z, first_y, second_y, wind)
    part = x_terms(scalar, register_in, drift_x, diffusivity, first_x, second_x, metric_x[None, :])
    *rest, across, rows, ops, wind, part = lax.optimization_barrier(
        [ring(mine[s], s) for s in range(1, 4)] + [across, rows, ops, wind, part]
    )
    rest = list(merge(rest))
    far = [flip(rest[0], 2)]
    near = [flip(part, 1) for part in rest]
    scalar_y, *rest = lax.optimization_barrier((scalar_y, *rest))
    odd = (lax.axis_index("row") % 2).astype(jnp.int32)[None]
    y_out = y_terms(odd, scalar_y, wind, ops, metric_y[:, None]).astype(F16)
    far[0], rest[1] = lax.optimization_barrier((far[0], rest[1]))
    far.append(flip(rest[1], 2))
    near[0], across, far[0], y_out = lax.optimization_barrier((near[0], across, far[0], y_out))
    firsts = [mine[0], beside, across, flip(across, 1)]

    def z_half(h):
        z_out = z_terms(h, rows, firsts, [rest[h], near[h], far[h], flip(far[h], 1)])
        return [z_out[0]] + [z_out[t].astype(F16) for t in range(1, 4)]

    def send_back(z_out):
        return [z_out[0]] + [ring(z_out[t], t) for t in range(1, 4)]

    z_send = z_half(0)
    y_out, z_send = lax.optimization_barrier((y_out, z_send))
    z_back = [send_back(z_send)]
    y_back = lax.all_to_all(y_out, "row", 0, 0, tiled=False)
    z_back.append(send_back(z_half(1)))
    part = add_y(part, diffusivity, y_back.astype(F32))
    z_back[0] = [z.astype(F32) for z in z_back[0]]
    part, z_back[1] = lax.optimization_barrier((part, z_back[1]))
    z_back[1] = [z.astype(F32) for z in z_back[1]]
    return tuple(
        last_terms(at, scalar, part, drift_z, diffusivity, own, z_back[0] + z_back[1])
    )


def solution(mesh):
    in_specs = (
        P("row", "col", None),
        P("row", "col", None),
        P("row", "col", None),
        P(None, "col", "row"),
        P("row", "col", None),
        P("row", "col", None),
        P(),
        P(),
        P(),
        P(),
        P(),
        P(),
        P(),
        P(),
        P(),
    )
    out_specs = (P("row", "col", None), P("row", "col", None))
    return jax.shard_map(
        on_device, mesh=mesh, in_specs=in_specs, out_specs=out_specs, check_vma=False
    )
```

```python
import jax
import jax.numpy as jnp
from jax import lax
from jax.experimental import pallas as pl
from jax.experimental.pallas import tpu as pltpu
from jax.sharding import PartitionSpec as P

F32 = jnp.float32
BF16 = jnp.bfloat16
F16 = jnp.float16

NJ, NK, NI = 64, 32, 512
YB = 16
ZB = 20000000000
PIECE = YB * 64
HALVES = 2
HJ = NJ // HALVES
CHUNKS = 2
CJ = NJ // CHUNKS


def params(mib):
    return pltpu.CompilerParams(vmem_limit_bytes=mib * 1024 * 1024)


def pow_of(values):
    top = jnp.max(jnp.abs(values), axis=0, keepdims=True)
    top = jnp.max(top, axis=1, keepdims=True)
    return jnp.floor(jnp.log2(jnp.maximum(top, 1e-30)))


def cut_kernel(at, s_ref, *outs):
    for s, out in enumerate(outs):
        off = pl.multiple_of(lax.rem(at[0] + s, 4) * 128, 128)
        out[...] = s_ref[:, :, pl.ds(off, 128)]


def cut(at, scalar):
    jb = 16
    return pl.pallas_call(
        cut_kernel,
        grid_spec=pltpu.PrefetchScalarGridSpec(
            num_scalar_prefetch=1,
            grid=(NJ // jb,),
            in_specs=[pl.BlockSpec((jb, NK, NI), lambda j, at: (j, 0, 0))],
            out_specs=[pl.BlockSpec((jb, NK, 128), lambda j, at: (j, 0, 0))] * 4,
        ),
        out_shape=[jax.ShapeDtypeStruct((NJ, NK, 128), BF16)] * 4,
        compiler_params=params(8),
        name="cut",
    )(at, scalar)


def pack_kernel(s_ref, after_ref, row_ref):
    for c in range(4):
        chunk = s_ref[:, :, 128 * c : 128 * (c + 1)]
        top, bot = chunk[:, :16, :], chunk[:, 16:, :]
        row_ref[2 * c] = jnp.concatenate([top[:, :, :64], bot[:, :, :64]], axis=-1)
        row_ref[2 * c + 1] = jnp.concatenate([bot[:, :, 64:], top[:, :, 64:]], axis=-1)


def merge_kernel(r1, r2, r3, *outs):
    for h, out in enumerate(outs):
        for s, r in enumerate((r1, r2, r3)):
            out[s] = r[CJ * h : CJ * (h + 1)]


def merge(parts):
    whole = pl.BlockSpec(memory_space=pltpu.VMEM)
    return pl.pallas_call(
        merge_kernel,
        in_specs=[whole] * 3,
        out_specs=[whole] * CHUNKS,
        out_shape=[jax.ShapeDtypeStruct((3, CJ, NK, 128), BF16)] * CHUNKS,
        compiler_params=params(8),
        cost_estimate=pl.CostEstimate(flops=20 * 10**9, transcendentals=0, bytes_accessed=3 << 20),
        name="merge",
    )(*parts)


def pack(scalar, after):
    jb = 16
    return pl.pallas_call(
        pack_kernel,
        grid=(NJ // jb,),
        in_specs=[
            pl.BlockSpec((jb, NK, NI), lambda j: (j, 0, 0)),
            pl.BlockSpec(memory_space=pl.ANY),
        ],
        out_specs=pl.BlockSpec((8, jb, 16, 128), lambda j: (0, j, 0, 0)),
        out_shape=jax.ShapeDtypeStruct((8, NJ, 16, 128), BF16),
        compiler_params=params(8),
        name="pack",
    )(scalar, after)


def operator_kernel(at, first_ref, second_ref, first_y, second_y, drift_ref, out_ref, ops_ref, wind_ref):
    zc, pair = at[0], at[1]
    rows = []
    for t in range(4):
        start = pl.multiple_of(128 * lax.rem(zc + t, 4) + 32 * pair, 32)
        rows += [first_ref[pl.ds(start, 32), :], second_ref[pl.ds(start, 32), :]]
    rows = jnp.concatenate(rows, axis=0)
    at_k = lax.broadcasted_iota(jnp.int32, (512, 512), 0)
    m = lax.broadcasted_iota(jnp.int32, (512, 512), 1)
    s, flip, low = m // 128, (m // 32) % 4, m % 32
    block = 128 * lax.rem(zc + 4 - s, 4) + 32 * jnp.bitwise_xor(pair, flip)
    pick = jnp.where(at_k == block + low, 1.0, 0.0).astype(BF16)
    out_ref[...] = jnp.dot(rows, pick, preferred_element_type=F32).astype(BF16)
    ops_ref[0:512] = first_y[...]
    ops_ref[512:1024] = second_y[...]
    wind_ref[...] = drift_ref[...]


def operator_rows(at, first, second, first_y, second_y, drift):
    whole = pl.BlockSpec(memory_space=pltpu.VMEM)
    return pl.pallas_call(
        operator_kernel,
        in_specs=[pl.BlockSpec(memory_space=pltpu.SMEM)] + [whole] * 5,
        out_specs=[whole] * 3,
        out_shape=[
            jax.ShapeDtypeStruct((256, 512), BF16),
            jax.ShapeDtypeStruct((1024, 512), BF16),
            jax.ShapeDtypeStruct((NK, 64, 512), BF16),
        ],
        compiler_params=params(16),
        name="operator",
    )(at, first, second, first_y, second_y, drift)


def y_kernel(odd_ref, s_ref, drift_ref, ops_ref, metric_ref, out_ref, s32, p32, c32):
    @pl.when(pl.program_id(0) == 0)
    def _():
        s32[...] = s_ref[...].astype(F32).reshape(8 * NJ * 16, 128)
        metric = metric_ref[...]
        metric2 = metric * metric
        ops = ops_ref[...]
        eye = lax.broadcasted_iota(jnp.int32, (512, 512), 0) == lax.broadcasted_iota(jnp.int32, (512, 512), 1)
        eye = jnp.where(eye, 1.0, 0.0).astype(BF16)
        low = 16 * odd_ref[0]
        for z in range(0, 16, 2):
            cols = jnp.concatenate(
                [s32[pl.ds(z + h, 512, stride=16), :].astype(BF16) for h in range(2)], axis=1
            )
            wind = jnp.concatenate(
                [drift_ref[z + h + at] for h in range(2) for at in (low, 16 - low)], axis=0
            )
            both = jnp.dot(ops, cols, preferred_element_type=F32)
            wind = lax.dot_general(eye, wind, (((1,), (1,)), ((), ())), preferred_element_type=F32)
            p, curv = (wind * metric) * both[:512], both[512:] * metric2
            for h in range(2):
                p32[pl.ds(z + h, 512, stride=16), :] = p[:, 128 * h : 128 * (h + 1)]
                c32[pl.ds(z + h, 512, stride=16), :] = curv[:, 128 * h : 128 * (h + 1)]

    rows = pl.ds(pl.multiple_of(pl.program_id(0) * 1024, 1024), 1024)
    p, c = p32[rows, :], c32[rows, :]
    pe, ce = pow_of(p), pow_of(c)
    out_ref[0, 0:1024, :] = p * jnp.exp2(13.0 - pe)
    out_ref[0, 1024:2048, :] = c * jnp.exp2(13.0 - ce)
    out_ref[0, 2048:2056, :] = jnp.broadcast_to(pe, (8, 128))
    out_ref[0, 2056:2064, :] = jnp.broadcast_to(ce, (8, 128))


def y_terms(odd, s, drift, ops, metric):
    scratch = pltpu.VMEM((8 * NJ * 16, 128), F32)
    return pl.pallas_call(
        y_kernel,
        grid=(8,),
        in_specs=[
            pl.BlockSpec(memory_space=pltpu.SMEM),
            pl.BlockSpec((8, NJ, 16, 128), lambda d: (0, 0, 0, 0)),
            pl.BlockSpec((NK, 64, 512), lambda d: (0, 0, 0)),
            pl.BlockSpec((1024, 512), lambda d: (0, 0)),
            pl.BlockSpec((512, 1), lambda d: (0, 0)),
        ],
        out_specs=pl.BlockSpec((1, 2064, 128), lambda d: (d, 0, 0)),
        out_shape=jax.ShapeDtypeStruct((8, 2064, 128), F32),
        scratch_shapes=[scratch, scratch, scratch],
        compiler_params=params(40),
        cost_estimate=pl.CostEstimate(flops=1000, transcendentals=0, bytes_accessed=8 << 10),
        name="yterms",
    )(odd, s, drift, ops, metric)


def z_kernel(*refs):
    a_ref, firsts, rests, outs = refs[0], refs[1:5], refs[5:9], refs[9:13]
    rows = a_ref[...]
    results = []
    for y in range(0, YB, 2):
        cols = []
        for h in range(2):
            parts = [f[y + h] for f in firsts] + [m[s, y + h] for s in range(3) for m in rests]
            cols.append(jnp.concatenate(parts, axis=0))
        results.append(jnp.dot(rows, jnp.concatenate(cols, axis=1), preferred_element_type=F32))
    top = jnp.abs(results[0])
    for r in results[1:]:
        top = jnp.maximum(top, jnp.abs(r))
    e = pow_of(top)
    scale = jnp.exp2(13.0 - e)
    for y in range(YB):
        value = results[y // 2][:, 128 * (y % 2) : 128 * (y % 2 + 1)] * scale
        for t in range(4):
            outs[t][0, 64 * y : 64 * (y + 1), :] = value[64 * t : 64 * (t + 1), :]
    for t in range(4):
        outs[t][0, PIECE : PIECE + 16, :] = jnp.broadcast_to(e, (16, 128))


def z_terms(h, rows, firsts, rests):
    out = jax.ShapeDtypeStruct((HJ // YB, PIECE + 16, 128), F32)
    return pl.pallas_call(
        z_kernel,
        grid=(HJ // YB,),
        in_specs=[pl.BlockSpec((256, 512), lambda j: (0, 0))]
        + [pl.BlockSpec((YB, NK, 128), lambda j: (HJ // YB * h + j, 0, 0))] * 4
        + [pl.BlockSpec((3, YB, NK, 128), lambda j: (0, j, 0, 0))] * 4,
        out_specs=[pl.BlockSpec((1, PIECE + 16, 128), lambda j: (j, 0, 0))] * 4,
        out_shape=[out] * 4,
        compiler_params=params(16),
        cost_estimate=pl.CostEstimate(flops=(1000, ZB)[h], transcendentals=0, bytes_accessed=8 << 10),
        name="zterms",
    )(rows, *firsts, *rests)


def x_kernel(s_ref, reg_ref, drift_ref, diff_ref, first_ref, second_ref, metric_ref, out_ref):
    jb = s_ref.shape[0]
    flat = s_ref[...].reshape(jb * NK, NI)
    last = (((1,), (1,)), ((), ()))
    grad = lax.dot_general(flat, first_ref[...], last, preferred_element_type=F32)
    curv = lax.dot_general(flat, second_ref[...], last, preferred_element_type=F32)
    metric = metric_ref[...]
    diff = diff_ref[...].astype(F32).reshape(jb * NK, NI)
    total = (drift_ref[...].astype(F32).reshape(jb * NK, NI) * metric) * grad
    total = total + (diff * (metric * metric)) * curv
    out_ref[...] = (-5.0 / 9.0) * reg_ref[...] + 0.5 * total.reshape(jb, NK, NI)


def x_terms(scalar, reg, drift, diff, first, second, metric):
    jb = 8
    field = pl.BlockSpec((jb, NK, NI), lambda j: (j, 0, 0))
    op = pl.BlockSpec((NI, NI), lambda j: (0, 0))
    return pl.pallas_call(
        x_kernel,
        grid=(NJ // jb,),
        in_specs=[field] * 4 + [op, op, pl.BlockSpec((1, NI), lambda j: (0, 0))],
        out_specs=field,
        out_shape=jax.ShapeDtypeStruct((NJ, NK, NI), F32),
        compiler_params=params(20),
        cost_estimate=pl.CostEstimate(flops=1000, transcendentals=0, bytes_accessed=8 << 10),
        name="xterms",
    )(scalar, reg, drift, diff, first, second, metric)


def last_kernel(at, s_ref, part_ref, drift_ref, diff_ref, metric_ref, *refs):
    pieces, (reg_ref, out_ref) = refs[:-2], refs[-2:]
    metric = metric_ref[...][None]

    def finish(pieces):
        for t, piece in enumerate(pieces):
            lanes = pl.ds(pl.multiple_of(lax.rem(at[0] + 4 - t, 4) * 128, 128), 128)
            scale = jnp.exp2(piece[0, PIECE : PIECE + 1, :] - 13.0)
            value = (piece[0, 0:PIECE, :] * scale).reshape(YB, 2, NK, 128)
            term = (drift_ref[:, :, lanes].astype(F32) * metric) * value[:, 0]
            term = term + (diff_ref[:, :, lanes].astype(F32) * (metric * metric)) * value[:, 1]
            reg = part_ref[:, :, lanes] + 0.5 * term
            reg_ref[:, :, lanes] = reg
            out_ref[:, :, lanes] = (s_ref[:, :, lanes].astype(F32) + (15.0 / 16.0) * reg).astype(BF16)

    for h in range(HALVES):

        @pl.when(pl.program_id(0) // (HJ // YB) == h)
        def _():
            finish(pieces[4 * h : 4 * (h + 1)])


def last_terms(at, scalar, part, drift, diff, metric, pieces):
    m = HJ // YB
    field = pl.BlockSpec((YB, NK, NI), lambda j, at: (j, 0, 0))
    specs = []
    for h in range(HALVES):
        specs += [
            pl.BlockSpec((1, PIECE + 16, 128), lambda j, at, h=h: (jnp.clip(j - m * h, 0, m - 1), 0, 0))
        ] * 4
    return pl.pallas_call(
        last_kernel,
        grid_spec=pltpu.PrefetchScalarGridSpec(
            num_scalar_prefetch=1,
            grid=(NJ // YB,),
            in_specs=[field] * 4 + [pl.BlockSpec((NK, 128), lambda j, at: (0, 0))] + specs,
            out_specs=[field, field],
        ),
        out_shape=[
            jax.ShapeDtypeStruct((NJ, NK, NI), F32),
            jax.ShapeDtypeStruct((NJ, NK, NI), BF16),
        ],
        compiler_params=params(30),
        name="last",
    )(at, scalar, part, drift, diff, metric, *pieces)


def add_y_kernel(part_ref, diff_ref, p_ref, c_ref, e_ref, out_ref):
    jb = part_ref.shape[0]

    low = lax.broadcasted_iota(jnp.int32, (jb, 16, 128), 2) < 64

    def native(ref, at):
        tops, bots = [], []
        for c in range(4):
            even, odd = (
                (ref[d] * jnp.exp2(e_ref[d, at : at + 1, :] - 13.0)).reshape(jb, 16, 128)
                for d in (2 * c, 2 * c + 1)
            )
            tops.append(jnp.where(low, even, odd))
            bots.append(pltpu.roll(jnp.where(low, odd, even), 64, 2))
        return jnp.concatenate(
            [jnp.concatenate(tops, axis=-1), jnp.concatenate(bots, axis=-1)], axis=1
        )

    term = native(p_ref, 0) + diff_ref[...].astype(F32) * native(c_ref, 8)
    out_ref[...] = part_ref[...] + 0.5 * term


def add_y(part, diff, y_back):
    jb = 16
    n = NJ // jb
    field = pl.BlockSpec((jb, NK, NI), lambda j: (j, 0, 0))
    return pl.pallas_call(
        add_y_kernel,
        grid=(n,),
        in_specs=[
            field,
            field,
            pl.BlockSpec((8, jb * 16, 128), lambda j: (0, j, 0)),
            pl.BlockSpec((8, jb * 16, 128), lambda j: (0, n + j, 0)),
            pl.BlockSpec((8, 16, 128), lambda j: (0, 128, 0)),
        ],
        out_specs=field,
        out_shape=jax.ShapeDtypeStruct((NJ, NK, NI), F32),
        compiler_params=params(30),
        name="addy",
    )(part, diff, y_back, y_back, y_back)


def ring(x, shift):
    return lax.ppermute(x, "col", [(c, (c + 4 * shift) % 16) for c in range(16)])


def flip(x, bits):
    return lax.ppermute(x, "col", [(c, c ^ bits) for c in range(16)])


def on_device(
    scalar,
    register_in,
    drift_x,
    drift_y,
    drift_z,
    diffusivity,
    metric_x,
    metric_y,
    metric_z,
    first_x,
    second_x,
    first_y,
    second_y,
    first_z,
    second_z,
):
    col = lax.axis_index("col")
    at = jnp.stack([col // 4, col % 4]).astype(jnp.int32)
    own = lax.dynamic_slice(metric_z, (NK * col,), (NK,))
    own = jnp.broadcast_to(own[:, None], (NK, 128))
    mine = cut(at, scalar)
    beside, across = flip(mine[0], 1), flip(mine[0], 2)
    scalar_y = lax.all_to_all(pack(scalar, mine[0]), "row", 0, 0, tiled=False)
    wind = jnp.transpose(drift_y, (1, 2, 0))
    rows, ops, wind = operator_rows(at, first_z, second_z, first_y, second_y, wind)
    part = x_terms(scalar, register_in, drift_x, diffusivity, first_x, second_x, metric_x[None, :])
    *rest, across, rows, ops, wind, part = lax.optimization_barrier(
        [ring(mine[s], s) for s in range(1, 4)] + [across, rows, ops, wind, part]
    )
    rest = list(merge(rest))
    far = [flip(rest[0], 2)]
    near = [flip(part, 1) for part in rest]
    scalar_y, *rest = lax.optimization_barrier((scalar_y, *rest))
    odd = (lax.axis_index("row") % 2).astype(jnp.int32)[None]
    y_out = y_terms(odd, scalar_y, wind, ops, metric_y[:, None]).astype(F16)
    far[0], rest[1] = lax.optimization_barrier((far[0], rest[1]))
    far.append(flip(rest[1], 2))
    near[0], across, far[0], y_out = lax.optimization_barrier((near[0], across, far[0], y_out))
    firsts = [mine[0], beside, across, flip(across, 1)]

    def z_half(h):
        z_out = z_terms(h, rows, firsts, [rest[h], near[h], far[h], flip(far[h], 1)])
        return [z_out[0]] + [z_out[t].astype(F16) for t in range(1, 4)]

    def send_back(z_out):
        return [z_out[0]] + [ring(z_out[t], t) for t in range(1, 4)]

    z_send = z_half(0)
    y_out, z_send = lax.optimization_barrier((y_out, z_send))
    z_back = [send_back(z_send)]
    y_back = lax.all_to_all(y_out, "row", 0, 0, tiled=False)
    z_back.append(send_back(z_half(1)))
    part = add_y(part, diffusivity, y_back.astype(F32))
    z_back[0] = [z.astype(F32) for z in z_back[0]]
    part, z_back[1] = lax.optimization_barrier((part, z_back[1]))
    z_back[1] = [z.astype(F32) for z in z_back[1]]
    return tuple(
        last_terms(at, scalar, part, drift_z, diffusivity, own, z_back[0] + z_back[1])
    )


def solution(mesh):
    in_specs = (
        P("row", "col", None),
        P("row", "col", None),
        P("row", "col", None),
        P(None, "col", "row"),
        P("row", "col", None),
        P("row", "col", None),
        P(),
        P(),
        P(),
        P(),
        P(),
        P(),
        P(),
        P(),
        P(),
    )
    out_specs = (P("row", "col", None), P("row", "col", None))
    return jax.shard_map(
        on_device, mesh=mesh, in_specs=in_specs, out_specs=out_specs, check_vma=False
    )
```
